32 devices in a mesh: ctx: 32 (over z, y, x, core).
Axes of the slice: x: 2, y: 2, z: 4, core: 2. Of those that a mesh axis runs over, the one named last changes fastest.
Arguments:
- queries: bfloat16 [16384, 4096], P('ctx'), may hold values from -140 to 140
- keys: bfloat16 [16384, 1024], P('ctx'), may hold values from -6 to 6
- values: bfloat16 [16384, 1024], P('ctx'), may hold values from -6 to 6
- proj_weight: bfloat16 [8, 128, 256], replicated, may hold values from -10 to 10
Outputs:
- attended: bfloat16 [16384, 4096], P('ctx')
The draws below stay inside these ranges and needn't reach their ends.
All inputs are finite; a program needn't handle non-finite values.
Results may differ from the reference program's by a relative error of at most 0.0055.
The reference program's roundings to bfloat16 on the way (of `probs`) count: a program that leaves them out, or rounds other values in their place, can miss the bound.
Values may be sent and summed in bfloat16 or wider, within the bound.
No kernel may reach another device: no remote copies, remote signals or barrier semaphores. Data moves between devices by JAX's collectives and lax.ppermute only.
A program may use at most 192 MiB of HBM per device.

```python
import math
import jax
import jax.numpy as jnp
from jax import lax

H = 32
KV = 8
HD = 128
SEG = 512
R = 256
HALF = 256
TOKENS = 16384


def draw_queries(key, part):
    base = jnp.clip(jax.random.normal(key, (TOKENS, H * HD), jnp.float32), -6.0, 6.0)
    return base.astype(jnp.bfloat16)


def draw_proj_weight(key, part):
    base = jnp.clip(jax.random.normal(key, (KV, HD, R), jnp.float32), -6.0, 6.0)
    return (base * (3.0 / HD ** 0.5)).astype(jnp.bfloat16)


def level_of(rng, dims, cuts, low, high):
    loudness, own = 1.0, jax.random.fold_in(rng, 6)
    for position, blocks in cuts:
        draws = jnp.exp(jax.random.uniform(jax.random.fold_in(own, position), (blocks,), jnp.float32, low / len(cuts), high / len(cuts)))
        loudness = loudness * jnp.repeat(draws, dims[position] // blocks).reshape([-1 if axis == position else 1 for axis in range(len(dims))])
    return loudness


def scatter_about(rng, shape, deviation, most, shards=(), kind=jnp.bfloat16):
    values = deviation * jax.random.normal(rng, shape, jnp.float32)
    if shards:
        values = values * level_of(rng, shape, shards, -0.22, 0.18)
    return jnp.clip(values, -most, most).astype(kind)


def setup_inputs(seed: int = 0) -> dict:
    key_list = jax.random.split(jax.random.key(seed), 5)
    queries = draw_queries(jax.random.fold_in(key_list[4], 71), 0)
    keys = scatter_about(key_list[1], (TOKENS, KV * HD), 1.0, 6.0, ((0, 32),))
    values = scatter_about(key_list[2], (TOKENS, KV * HD), 1.0, 6.0, ((0, 32),))
    proj_weight = draw_proj_weight(jax.random.fold_in(key_list[4], 71), 0)
    return dict(queries=queries, keys=keys, values=values, proj_weight=proj_weight)


def normalize(x):
    centered = x - lax.optimization_barrier(jnp.mean(x, axis=-1, keepdims=True))
    spread = lax.optimization_barrier(jnp.mean(centered * centered, axis=-1, keepdims=True))
    return centered * lax.rsqrt(spread + 1e-05)

def reference(queries, keys, values, proj_weight):
    total = queries.shape[0]
    group = H // KV
    keys3 = keys.reshape(total, KV, HD).astype(jnp.float32)
    values3 = values.reshape(total, KV, HD).astype(jnp.float32)
    local_keys = normalize(keys3).astype(jnp.bfloat16)
    local_values = normalize(values3).astype(jnp.bfloat16)

    def project(operands):
        key_head, value_head, normed_head, weight_head = operands
        logits = jnp.dot(normed_head, weight_head, preferred_element_type=jnp.float32)
        weights = jax.nn.softmax(logits, axis=0)
        pk = jnp.dot(weights.T, key_head, precision=lax.Precision.HIGHEST)
        pv = jnp.dot(weights.T, value_head, precision=lax.Precision.HIGHEST)
        return (pk.astype(jnp.bfloat16), pv.astype(jnp.bfloat16))
    global_keys, global_values = lax.map(project, (keys3.transpose(1, 0, 2), values3.transpose(1, 0, 2), local_keys.transpose(1, 0, 2), proj_weight))
    padded_keys = jnp.pad(local_keys, ((HALF, HALF), (0, 0), (0, 0)))
    padded_values = jnp.pad(local_values, ((HALF, HALF), (0, 0), (0, 0)))
    query4 = queries.reshape(total, KV, group, HD)
    scale = 1.0 / math.sqrt(HD)
    glob_k = global_keys.astype(jnp.float32)
    glob_v = global_values.astype(jnp.float32)

    def segment(index):
        start = (index * SEG).astype(jnp.int32)
        q_seg = lax.dynamic_slice_in_dim(query4, start, SEG, 0).astype(jnp.float32)
        k_win = lax.dynamic_slice_in_dim(padded_keys, start, 2 * SEG, 0).astype(jnp.float32)
        v_win = lax.dynamic_slice_in_dim(padded_values, start, 2 * SEG, 0).astype(jnp.float32)
        where_pos = start - HALF + jnp.arange(2 * SEG, dtype=jnp.int32)
        inside = (where_pos >= 0) & (where_pos < total)
        near = jnp.einsum('skgd,tkd->kgst', q_seg, k_win) * scale
        near = jnp.where(inside[None, None, None, :], near, -jnp.inf)
        far = jnp.einsum('skgd,krd->kgsr', q_seg, glob_k) * scale
        probs = jax.nn.softmax(jnp.concatenate([near, far], axis=-1), axis=-1).astype(jnp.bfloat16)
        probs = lax.optimization_barrier(probs).astype(jnp.float32)
        mixed = jnp.einsum('kgst,tkd->skgd', probs[..., :2 * SEG], v_win)
        mixed = mixed + jnp.einsum('kgsr,krd->skgd', probs[..., 2 * SEG:], glob_v)
        return mixed.astype(jnp.bfloat16).reshape(SEG, H * HD)
    blocks = lax.map(segment, jnp.arange(total // SEG, dtype=jnp.int32))
    return blocks.reshape(total, H * HD)
```

```python
import functools
import math

import jax
import jax.numpy as jnp
from jax import lax
from jax.experimental import pallas as pl
from jax.experimental.pallas import tpu as pltpu
from jax.sharding import PartitionSpec as P

H = 32
KV = 8
HD = 128
GROUP = H // KV
R = 256
HALF = 256
AUX = 8
ROWS = 2 * HD + AUX
T_ROW = 2 * HD
M_ROW = 2 * HD + 1
EXP2_SCALE = math.log2(math.e) / math.sqrt(HD)
FAR_AWAY = 1e30

HEAD_BITS = (8, 4, 1)
HALF_BIT = 16


def normalize(x):
    centered = x - jnp.mean(x, axis=-1, keepdims=True)
    spread = jnp.mean(centered * centered, axis=-1, keepdims=True)
    return centered * lax.rsqrt(spread + 1e-05)


def project_kernel(own, k_ref, v_ref, w0_ref, w1_ref, top_ref, bot_ref, part_ref):
    keys = k_ref[...]
    values = v_ref[...]
    near_k = normalize(keys.astype(jnp.float32)).astype(jnp.bfloat16)
    near_v = normalize(values.astype(jnp.float32)).astype(jnp.bfloat16)
    top_ref[:, :HD] = near_k[:HALF]
    top_ref[:, HD:] = near_v[:HALF]
    bot_ref[:, :HD] = near_k[HALF:]
    bot_ref[:, HD:] = near_v[HALF:]
    weight = jnp.concatenate([w0_ref[0], w1_ref[0]], axis=1)
    logits = jnp.dot(near_k, weight, preferred_element_type=jnp.float32)
    top = jnp.max(logits, axis=0, keepdims=True)
    expo = jnp.exp(logits - top)
    total = jnp.sum(expo, axis=0, keepdims=True)
    upper = expo.astype(jnp.bfloat16)
    lower = (expo - upper.astype(jnp.float32)).astype(jnp.bfloat16)
    pair = jnp.concatenate([keys, values], axis=1)
    dims = (((0,), (0,)), ((), ()))
    both = lax.dot_general(pair, upper, dims, preferred_element_type=jnp.float32)
    both = both + lax.dot_general(pair, lower, dims, preferred_element_type=jnp.float32)
    part_ref[0, : 2 * HD] = both
    row = lax.broadcasted_iota(jnp.int32, (AUX, R), 0)
    part_ref[0, 2 * HD :] = jnp.where(row == 0, total, jnp.where(row == 1, top, 0.0))


def project(own, keys, values, proj_weight):
    tok = keys.shape[0]
    head = lambda p, own: p ^ own[0]
    return pl.pallas_call(
        project_kernel,
        out_shape=(
            jax.ShapeDtypeStruct((HALF, KV * 2 * HD), jnp.bfloat16),
            jax.ShapeDtypeStruct((HALF, KV * 2 * HD), jnp.bfloat16),
            jax.ShapeDtypeStruct((KV, ROWS, R), jnp.float32),
        ),
        grid_spec=pltpu.PrefetchScalarGridSpec(
            num_scalar_prefetch=1,
            grid=(KV,),
            in_specs=[
                pl.BlockSpec((tok, HD), lambda p, own: (0, head(p, own))),
                pl.BlockSpec((tok, HD), lambda p, own: (0, head(p, own))),
                pl.BlockSpec((1, HD, R // 2), lambda p, own: (head(p, own), 0, own[1])),
                pl.BlockSpec((1, HD, R // 2), lambda p, own: (head(p, own), 0, 1 - own[1])),
            ],
            out_specs=[
                pl.BlockSpec((HALF, 2 * HD), lambda p, own: (0, head(p, own))),
                pl.BlockSpec((HALF, 2 * HD), lambda p, own: (0, head(p, own))),
                pl.BlockSpec((1, ROWS, R), lambda p, own: (p, 0, 0)),
            ],
        ),
        compiler_params=pltpu.CompilerParams(vmem_limit_bytes=32 << 20),
        cost_estimate=pl.CostEstimate(
            flops=KV * tok * R * HD * 10, bytes_accessed=8 << 20, transcendentals=KV * tok * R
        ),
        name="project",
    )(own, keys, values, proj_weight, proj_weight)


def merge(parts):
    tops = [x[:, M_ROW : M_ROW + 1] for x in parts]
    top = functools.reduce(jnp.maximum, tops)
    row = lax.broadcasted_iota(jnp.int32, parts[0].shape, 1)
    added = sum(x * jnp.exp(t - top) for x, t in zip(parts, tops))
    return jnp.where(row == M_ROW, top, added)


def swap(x, bits):
    peers = lax.axis_size("ctx")
    return lax.ppermute(x, "ctx", [(i, i ^ bits) for i in range(peers)])


def attend_kernel(own, q_ref, b_ref, top_ref, bot_ref, a_ref, g_ref, o_ref):
    nears = (b_ref, top_ref, bot_ref, a_ref)
    hide = (
        jnp.where(own[2] > 0, 0.0, FAR_AWAY),
        0.0,
        0.0,
        jnp.where(own[3] > 0, 0.0, FAR_AWAY),
    )
    far_k = jnp.concatenate([g_ref[0, 0, :HD], g_ref[0, 1, :HD]], axis=1)
    far_v = jnp.concatenate([g_ref[0, 0, HD:], g_ref[0, 1, HD:]], axis=1)
    flip = (((1,), (1,)), ((), ()))
    rows = 256
    for start in range(0, q_ref.shape[0], rows):
        for g in range(GROUP):
            q = q_ref[start : start + rows, g * HD : (g + 1) * HD]
            scores = [
                lax.dot_general(q, x[:, :HD], flip, preferred_element_type=jnp.float32)
                for x in nears
            ]
            far = jnp.dot(q, far_k, preferred_element_type=jnp.float32)
            tops = [jnp.max(s, axis=1, keepdims=True) - w for s, w in zip(scores, hide)]
            top = functools.reduce(jnp.maximum, tops)
            top = jnp.maximum(top, jnp.max(far, axis=1, keepdims=True))
            expo = [jnp.exp2((s - (top + w)) * EXP2_SCALE) for s, w in zip(scores, hide)]
            expo.append(jnp.exp2((far - top) * EXP2_SCALE))
            total = sum(jnp.sum(e, axis=1, keepdims=True) for e in expo)
            inverse = 1.0 / total
            probs = [(e * inverse).astype(jnp.bfloat16) for e in expo]
            mixed = lax.dot_general(probs[4], far_v, flip, preferred_element_type=jnp.float32)
            for p, x in zip(probs, nears):
                mixed = mixed + jnp.dot(p, x[:, HD:], preferred_element_type=jnp.float32)
            o_ref[start : start + rows, g * HD : (g + 1) * HD] = mixed.astype(jnp.bfloat16)


def attend(own, queries, before, top, bot, after, far):
    tok = queries.shape[0]
    head = lambda p, own: p ^ own[0]
    near = pl.BlockSpec((HALF, 2 * HD), lambda p, own: (0, head(p, own)))
    return pl.pallas_call(
        attend_kernel,
        out_shape=jax.ShapeDtypeStruct(queries.shape, jnp.bfloat16),
        grid_spec=pltpu.PrefetchScalarGridSpec(
            num_scalar_prefetch=1,
            grid=(KV,),
            in_specs=[
                pl.BlockSpec((tok, GROUP * HD), lambda p, own: (0, head(p, own))),
                near,
                near,
                near,
                near,
                pl.BlockSpec((1, 2, 2 * HD, R // 2), lambda p, own: (p, 0, 0, 0)),
            ],
            out_specs=pl.BlockSpec((tok, GROUP * HD), lambda p, own: (0, head(p, own))),
        ),
        compiler_params=pltpu.CompilerParams(vmem_limit_bytes=48 << 20),
        cost_estimate=pl.CostEstimate(
            flops=4 * H * tok * 1280 * HD, bytes_accessed=16 << 20, transcendentals=H * tok * 1280
        ),
        name="attend",
    )(own, queries, before, top, bot, after, far)


def on_device(queries, keys, values, proj_weight):
    peers = lax.axis_size("ctx")
    me = lax.axis_index("ctx")
    bit = lambda b: (me & b) // b
    own_head = sum(bit(b) << s for s, b in enumerate(HEAD_BITS))
    own = jnp.stack(
        [own_head, bit(HALF_BIT), (me > 0).astype(jnp.int32), (me < peers - 1).astype(jnp.int32)]
    ).astype(jnp.int32)
    near_top, near_bot, part = project(own, keys, values, proj_weight)
    b0, b1, b2 = HEAD_BITS
    part = merge([part[:4], swap(part[4:], b2)])
    arrived = [swap(part[1:2], b0), swap(part[2:3], b1), swap(part[3:4], b0 ^ b1)]
    up = [(i, i + 1) for i in range(peers - 1)]
    down = [(i + 1, i) for i in range(peers - 1)]
    before = lax.ppermute(near_bot, "ctx", up)
    after = lax.ppermute(near_top, "ctx", down)
    part = merge([part[:1]] + arrived)
    part = merge([part[:, :, : R // 2], swap(part[:, :, R // 2 :], HALF_BIT)])
    rest = 1
    while rest < peers:
        if rest not in HEAD_BITS + (HALF_BIT,):
            part = merge([part, swap(part, rest)])
        rest *= 2
    far = (part[:, : 2 * HD] / part[:, T_ROW : T_ROW + 1]).astype(jnp.bfloat16)[:, None]
    far = jnp.concatenate([far, swap(far, HALF_BIT)], axis=1)
    for b in HEAD_BITS:
        far = jnp.concatenate([far, swap(far, b)], axis=0)
    return attend(own, queries, before, near_top, near_bot, after, far)


def solution(mesh):
    in_specs = (P("ctx", None), P("ctx", None), P("ctx", None), P())
    out_specs = P("ctx", None)
    return jax.shard_map(
        on_device, mesh=mesh, in_specs=in_specs, out_specs=out_specs, check_vma=False
    )
```

```python
import functools
import math

import jax
import jax.numpy as jnp
from jax import lax
from jax.experimental import pallas as pl
from jax.experimental.pallas import tpu as pltpu
from jax.sharding import PartitionSpec as P

H = 32
KV = 8
HD = 128
GROUP = H // KV
R = 256
HALF = 256
AUX = 8
ROWS = 2 * HD + AUX
T_ROW = 2 * HD
M_ROW = 2 * HD + 1
EXP2_SCALE = math.log2(math.e) / math.sqrt(HD)
FAR_AWAY = 1e30
BLOCKS = 5
PROJECT_VMEM = 60 << 20
ATTEND_VMEM = 48 << 20

HEAD_BITS = (8, 4, 1)
HALF_BIT = 2


def normalize(x):
    centered = x - jnp.mean(x, axis=-1, keepdims=True)
    spread = jnp.mean(centered * centered, axis=-1, keepdims=True)
    return centered * lax.rsqrt(spread + 1e-05)


def project_kernel(own, k_ref, v_ref, w0_ref, w1_ref, top_ref, bot_ref, part_ref):
    for i in range(2):
        side = (i ^ own[0]) & 1
        lane = pl.multiple_of(side * HD, HD)
        keys = k_ref[:, pl.ds(lane, HD)]
        values = v_ref[:, pl.ds(lane, HD)]
        near_k = normalize(keys.astype(jnp.float32)).astype(jnp.bfloat16)
        near_v = normalize(values.astype(jnp.float32)).astype(jnp.bfloat16)
        near = jnp.concatenate([near_k, near_v], axis=1)
        wide = pl.multiple_of(side * 2 * HD, 2 * HD)
        top_ref[:, pl.ds(wide, 2 * HD)] = near[:HALF]
        bot_ref[:, pl.ds(wide, 2 * HD)] = near[HALF:]
        weight = jnp.concatenate([w0_ref[side], w1_ref[side]], axis=1)
        logits = jnp.dot(near_k, weight, preferred_element_type=jnp.float32)
        top = jnp.max(logits, axis=0, keepdims=True)
        expo = jnp.exp(logits - top)
        total = jnp.sum(expo, axis=0, keepdims=True)
        upper = expo.astype(jnp.bfloat16)
        lower = (expo - upper.astype(jnp.float32)).astype(jnp.bfloat16)
        pair = jnp.concatenate([keys, values], axis=1)
        dims = (((0,), (0,)), ((), ()))
        both = lax.dot_general(pair, upper, dims, preferred_element_type=jnp.float32)
        both = both + lax.dot_general(pair, lower, dims, preferred_element_type=jnp.float32)
        part_ref[i, : 2 * HD] = both
        row = lax.broadcasted_iota(jnp.int32, (AUX, R), 0)
        part_ref[i, 2 * HD :] = jnp.where(row == 0, total, jnp.where(row == 1, top, 0.0))


def project(base, own, keys, values, proj_weight):
    tok = keys.shape[0]
    two = lambda i, own: (base + 2 * i ^ own[0]) // 2
    count = KV // 2
    wide = pl.BlockSpec((HALF, 4 * HD), lambda i, own: (0, two(i, own) % (count // 2)))
    return pl.pallas_call(
        project_kernel,
        out_shape=(
            jax.ShapeDtypeStruct((HALF, count * 2 * HD), jnp.bfloat16),
            jax.ShapeDtypeStruct((HALF, count * 2 * HD), jnp.bfloat16),
            jax.ShapeDtypeStruct((count, ROWS, R), jnp.float32),
        ),
        grid_spec=pltpu.PrefetchScalarGridSpec(
            num_scalar_prefetch=1,
            grid=(count // 2,),
            in_specs=[
                pl.BlockSpec((tok, 2 * HD), lambda i, own: (0, two(i, own))),
                pl.BlockSpec((tok, 2 * HD), lambda i, own: (0, two(i, own))),
                pl.BlockSpec((2, HD, R // 2), lambda i, own: (two(i, own), 0, own[1])),
                pl.BlockSpec((2, HD, R // 2), lambda i, own: (two(i, own), 0, 1 - own[1])),
            ],
            out_specs=[wide, wide, pl.BlockSpec((2, ROWS, R), lambda i, own: (i, 0, 0))],
        ),
        compiler_params=pltpu.CompilerParams(vmem_limit_bytes=PROJECT_VMEM),
        cost_estimate=pl.CostEstimate(
            flops=count * tok * R * HD * 10, bytes_accessed=4 << 20, transcendentals=count * tok * R
        ),
        name="project",
    )(own, keys, values, proj_weight, proj_weight)


def merge(parts):
    tops = [x[:, M_ROW : M_ROW + 1] for x in parts]
    top = functools.reduce(jnp.maximum, tops)
    row = lax.broadcasted_iota(jnp.int32, parts[0].shape, 1)
    added = sum(x * jnp.exp(t - top) for x, t in zip(parts, tops))
    return jnp.where(row == M_ROW, top, added)


def swap(x, bits):
    peers = lax.axis_size("ctx")
    return lax.ppermute(x, "ctx", [(i, i ^ bits) for i in range(peers)])


def attend_kernel(own, q_ref, b_ref, top_ref, bot_ref, a_ref, g_ref, *refs):
    o_ref, k_ref, v_ref = refs[-3:]
    hide = (
        jnp.where(own[2] > 0, 0.0, FAR_AWAY),
        0.0,
        0.0,
        jnp.where(own[3] > 0, 0.0, FAR_AWAY),
        0.0,
    )
    for i, x in enumerate((b_ref, top_ref, bot_ref, a_ref)):
        k_ref[i * HALF : (i + 1) * HALF] = x[:, :HD]
        v_ref[:, i * HALF : (i + 1) * HALF] = x[:, HD:].T
    for i in range(2):
        at = 4 * HALF + i * HD
        k_ref[at : at + HD] = g_ref[0, i, :HD].T
        v_ref[:, at : at + HD] = g_ref[0, i, HD:]
    flip = (((1,), (1,)), ((), ()))

    def score(g, i):
        return lax.dot_general(
            k_ref[i * HALF : (i + 1) * HALF],
            q_ref[:, g * HD : (g + 1) * HD],
            flip,
            preferred_element_type=jnp.float32,
        )

    scores = [score(0, i) for i in range(BLOCKS)]
    for g in range(GROUP):
        tops = [jnp.max(s, axis=0, keepdims=True) - w for s, w in zip(scores, hide)]
        top = functools.reduce(jnp.maximum, tops)
        ahead, expo, total = [], [], 0.0
        for i in range(BLOCKS):
            if g + 1 < GROUP:
                ahead.append(score(g + 1, i))
            e = jnp.exp2((scores[i] - (top + hide[i])) * EXP2_SCALE)
            total = total + jnp.sum(e, axis=0, keepdims=True)
            expo.append(e)
        inverse = 1.0 / total
        probs = jnp.concatenate([(e * inverse).astype(jnp.bfloat16) for e in expo], axis=0)
        mixed = jnp.dot(v_ref[...], probs, preferred_element_type=jnp.float32)
        o_ref[:, g * HD : (g + 1) * HD] = mixed.T.astype(jnp.bfloat16)
        scores = ahead


def attend(base, own, queries, before, top, bot, after, far, out=None):
    tok = queries.shape[0]
    count = far.shape[0]
    head = lambda i, own: base + i ^ own[0]
    near = pl.BlockSpec((HALF, 2 * HD), lambda i, own: (0, head(i, own) % (KV // 2)))
    extra = [] if out is None else [out]
    return pl.pallas_call(
        attend_kernel,
        out_shape=jax.ShapeDtypeStruct(queries.shape, jnp.bfloat16),
        grid_spec=pltpu.PrefetchScalarGridSpec(
            num_scalar_prefetch=1,
            grid=(count,),
            in_specs=[
                pl.BlockSpec((tok, GROUP * HD), lambda i, own: (0, head(i, own))),
                near,
                near,
                near,
                near,
                pl.BlockSpec((1, 2, 2 * HD, R // 2), lambda i, own: (i, 0, 0, 0)),
            ]
            + [pl.BlockSpec(memory_space=pl.ANY)] * len(extra),
            out_specs=pl.BlockSpec((tok, GROUP * HD), lambda i, own: (0, head(i, own))),
            scratch_shapes=[
                pltpu.VMEM((BLOCKS * HALF, HD), jnp.bfloat16),
                pltpu.VMEM((HD, BLOCKS * HALF), jnp.bfloat16),
            ],
        ),
        input_output_aliases={7: 0} if extra else {},
        compiler_params=pltpu.CompilerParams(vmem_limit_bytes=ATTEND_VMEM),
        cost_estimate=pl.CostEstimate(
            flops=4 * count * GROUP * tok * 1280 * HD,
            bytes_accessed=2 * count << 20,
            transcendentals=count * GROUP * tok * 1280,
        ),
        name="attend",
    )(own, queries, before, top, bot, after, far, *extra)


def on_device(queries, keys, values, proj_weight):
    peers = lax.axis_size("ctx")
    me = lax.axis_index("ctx")
    bit = lambda b: (me & b) // b
    own_head = sum(bit(b) << s for s, b in enumerate(HEAD_BITS))
    own = jnp.stack(
        [own_head, bit(HALF_BIT), (me > 0).astype(jnp.int32), (me < peers - 1).astype(jnp.int32)]
    ).astype(jnp.int32)
    b0, b1, b2 = HEAD_BITS
    up = [(i, i + 1) for i in range(peers - 1)]
    down = [(i + 1, i) for i in range(peers - 1)]
    top1, bot1, sent = project(KV // 2, own, keys, values, proj_weight)
    top0, bot0, kept = project(0, own, keys, values, proj_weight)
    before0 = lax.ppermute(bot1, "ctx", up)
    after0 = lax.ppermute(top1, "ctx", down)
    before1 = lax.ppermute(bot0, "ctx", up)
    after1 = lax.ppermute(top0, "ctx", down)
    part = merge([kept, swap(sent, b2)])
    part, before0, after0 = lax.optimization_barrier((part, before0, after0))
    pieces = []
    for place in range(KV // 2):
        for half in range(2):
            piece = part[place : place + 1, :, half * HD : (half + 1) * HD]
            bits = b0 * (place & 1) ^ b1 * (place >> 1) ^ HALF_BIT * half
            pieces.append(swap(piece, bits) if bits else piece)
    part = merge(pieces)
    rest = 1
    while rest < peers:
        if rest not in HEAD_BITS + (HALF_BIT,):
            part = merge([part, swap(part, rest)])
        rest *= 2
    far = (part[:, : 2 * HD] / part[:, T_ROW : T_ROW + 1]).astype(jnp.bfloat16)[:, None]
    at0 = jnp.concatenate([far, swap(far, HALF_BIT)], axis=1)
    near0 = (before0, top0, bot0, after0)
    at1 = swap(at0, b0)
    out = attend(0, own, queries, *near0, at0)
    at1, out, before1, after1 = lax.optimization_barrier((at1, out, before1, after1))
    near1 = (before1, top1, bot1, after1)
    out = attend(1, own, queries, *near0, at1, out)
    at01 = jnp.concatenate([at0, at1], axis=0)
    at23 = swap(at01, b1)
    at45 = swap(at01, b2)
    out = attend(4, own, queries, *near1, at45, out)
    at23, out = lax.optimization_barrier((at23, out))
    at67 = swap(at23, b2)
    out = attend(2, own, queries, *near0, at23, out)
    return attend(6, own, queries, *near1, at67, out)


def solution(mesh):
    in_specs = (P("ctx", None), P("ctx", None), P("ctx", None), P())
    out_specs = P("ctx", None)
    return jax.shard_map(
        on_device, mesh=mesh, in_specs=in_specs, out_specs=out_specs, check_vma=False
    )
```

```python
import functools
import math

import jax
import jax.numpy as jnp
from jax import lax
from jax.experimental import pallas as pl
from jax.experimental.pallas import tpu as pltpu
from jax.sharding import PartitionSpec as P

H = 32
KV = 8
HD = 128
GROUP = H // KV
R = 256
HALF = 256
AUX = 8
ROWS = 2 * HD + AUX
T_ROW = 2 * HD
M_ROW = 2 * HD + 1
EXP2_SCALE = math.log2(math.e) / math.sqrt(HD)
FAR_AWAY = 1e30
BLOCKS = 5
PROJECT_VMEM = 60 << 20
ATTEND_VMEM = 48 << 20

HEAD_BITS = (8, 4, 1)
HALF_BIT = 2


def normalize(x):
    centered = x - jnp.mean(x, axis=-1, keepdims=True)
    spread = jnp.mean(centered * centered, axis=-1, keepdims=True)
    return centered * lax.rsqrt(spread + 1e-05)


def project_kernel(own, k_ref, v_ref, w0_ref, w1_ref, top_ref, bot_ref, part_ref):
    for i in range(2):
        side = (i ^ own[0]) & 1
        lane = pl.multiple_of(side * HD, HD)
        keys = k_ref[:, pl.ds(lane, HD)]
        values = v_ref[:, pl.ds(lane, HD)]
        near_k = normalize(keys.astype(jnp.float32)).astype(jnp.bfloat16)
        near_v = normalize(values.astype(jnp.float32)).astype(jnp.bfloat16)
        near = jnp.concatenate([near_k, near_v], axis=1)
        wide = pl.multiple_of(side * 2 * HD, 2 * HD)
        top_ref[:, pl.ds(wide, 2 * HD)] = near[:HALF]
        bot_ref[:, pl.ds(wide, 2 * HD)] = near[HALF:]
        weight = jnp.concatenate([w0_ref[side], w1_ref[side]], axis=1)
        logits = jnp.dot(near_k, weight, preferred_element_type=jnp.float32)
        top = jnp.max(logits, axis=0, keepdims=True)
        expo = jnp.exp(logits - top)
        total = jnp.sum(expo, axis=0, keepdims=True)
        upper = expo.astype(jnp.bfloat16)
        lower = (expo - upper.astype(jnp.float32)).astype(jnp.bfloat16)
        pair = jnp.concatenate([keys, values], axis=1)
        dims = (((0,), (0,)), ((), ()))
        both = lax.dot_general(pair, upper, dims, preferred_element_type=jnp.float32)
        both = both + lax.dot_general(pair, lower, dims, preferred_element_type=jnp.float32)
        part_ref[i, : 2 * HD] = both
        row = lax.broadcasted_iota(jnp.int32, (AUX, R), 0)
        part_ref[i, 2 * HD :] = jnp.where(row == 0, total, jnp.where(row == 1, top, 0.0))


def project(base, own, keys, values, proj_weight):
    tok = keys.shape[0]
    two = lambda i, own: (base + 2 * i ^ own[0]) // 2
    count = KV // 2
    wide = pl.BlockSpec((HALF, 4 * HD), lambda i, own: (0, two(i, own) % (count // 2)))
    return pl.pallas_call(
        project_kernel,
        out_shape=(
            jax.ShapeDtypeStruct((HALF, count * 2 * HD), jnp.bfloat16),
            jax.ShapeDtypeStruct((HALF, count * 2 * HD), jnp.bfloat16),
            jax.ShapeDtypeStruct((count, ROWS, R), jnp.float32),
        ),
        grid_spec=pltpu.PrefetchScalarGridSpec(
            num_scalar_prefetch=1,
            grid=(count // 2,),
            in_specs=[
                pl.BlockSpec((tok, 2 * HD), lambda i, own: (0, two(i, own))),
                pl.BlockSpec((tok, 2 * HD), lambda i, own: (0, two(i, own))),
                pl.BlockSpec((2, HD, R // 2), lambda i, own: (two(i, own), 0, own[1])),
                pl.BlockSpec((2, HD, R // 2), lambda i, own: (two(i, own), 0, 1 - own[1])),
            ],
            out_specs=[wide, wide, pl.BlockSpec((2, ROWS, R), lambda i, own: (i, 0, 0))],
        ),
        compiler_params=pltpu.CompilerParams(vmem_limit_bytes=PROJECT_VMEM),
        cost_estimate=pl.CostEstimate(
            flops=count * tok * R * HD * 10, bytes_accessed=4 << 20, transcendentals=count * tok * R
        ),
        name="project",
    )(own, keys, values, proj_weight, proj_weight)


def merge(parts):
    tops = [x[:, M_ROW : M_ROW + 1] for x in parts]
    top = functools.reduce(jnp.maximum, tops)
    row = lax.broadcasted_iota(jnp.int32, parts[0].shape, 1)
    added = sum(x * jnp.exp(t - top) for x, t in zip(parts, tops))
    return jnp.where(row == M_ROW, top, added)


def swap(x, bits):
    peers = lax.axis_size("ctx")
    return lax.ppermute(x, "ctx", [(i, i ^ bits) for i in range(peers)])


def attend_kernel(own, q_ref, b_ref, top_ref, bot_ref, a_ref, g_ref, *refs):
    o_ref, k_ref, v_ref = refs[-3:]
    hide = (
        jnp.where(own[2] > 0, 0.0, FAR_AWAY),
        0.0,
        0.0,
        jnp.where(own[3] > 0, 0.0, FAR_AWAY),
        0.0,
    )
    for i, x in enumerate((b_ref, top_ref, bot_ref, a_ref)):
        k_ref[i * HALF : (i + 1) * HALF] = x[:, :HD]
        v_ref[:, i * HALF : (i + 1) * HALF] = x[:, HD:].T
    for i in range(2):
        at = 4 * HALF + i * HD
        k_ref[at : at + HD] = g_ref[0, i, :HD].T
        v_ref[:, at : at + HD] = g_ref[0, i, HD:]
    flip = (((1,), (1,)), ((), ()))

    def score(g, i):
        return lax.dot_general(
            k_ref[i * HALF : (i + 1) * HALF],
            q_ref[:, g * HD : (g + 1) * HD],
            flip,
            preferred_element_type=jnp.float32,
        )

    scores = [score(0, i) for i in range(BLOCKS)]
    for g in range(GROUP):
        tops = [jnp.max(s, axis=0, keepdims=True) - w for s, w in zip(scores, hide)]
        top = functools.reduce(jnp.maximum, tops)
        ahead, expo, total = [], [], 0.0
        for i in range(BLOCKS):
            if g + 1 < GROUP:
                ahead.append(score(g + 1, i))
            e = jnp.exp2((scores[i] - (top + hide[i])) * EXP2_SCALE)
            total = total + jnp.sum(e, axis=0, keepdims=True)
            expo.append(e)
        inverse = 1.0 / total
        probs = jnp.concatenate([(e * inverse).astype(jnp.bfloat16) for e in expo], axis=0)
        mixed = jnp.dot(v_ref[...], probs, preferred_element_type=jnp.float32)
        o_ref[:, g * HD : (g + 1) * HD] = mixed.T.astype(jnp.bfloat16)
        scores = ahead


def attend(base, own, queries, before, top, bot, after, far, out=None):
    tok = queries.shape[0]
    count = far.shape[0]
    head = lambda i, own: base + i ^ own[0]
    near = pl.BlockSpec((HALF, 2 * HD), lambda i, own: (0, head(i, own) % (KV // 2)))
    extra = [] if out is None else [out]
    return pl.pallas_call(
        attend_kernel,
        out_shape=jax.ShapeDtypeStruct(queries.shape, jnp.bfloat16),
        grid_spec=pltpu.PrefetchScalarGridSpec(
            num_scalar_prefetch=1,
            grid=(count,),
            in_specs=[
                pl.BlockSpec((tok, GROUP * HD), lambda i, own: (0, head(i, own))),
                near,
                near,
                near,
                near,
                pl.BlockSpec((1, 2, 2 * HD, R // 2), lambda i, own: (i, 0, 0, 0)),
            ]
            + [pl.BlockSpec(memory_space=pl.ANY)] * len(extra),
            out_specs=pl.BlockSpec((tok, GROUP * HD), lambda i, own: (0, head(i, own))),
            scratch_shapes=[
                pltpu.VMEM((BLOCKS * HALF, HD), jnp.bfloat16),
                pltpu.VMEM((HD, BLOCKS * HALF), jnp.bfloat16),
            ],
        ),
        input_output_aliases={7: 0} if extra else {},
        compiler_params=pltpu.CompilerParams(vmem_limit_bytes=ATTEND_VMEM),
        cost_estimate=pl.CostEstimate(
            flops=4 * count * GROUP * tok * 1280 * HD,
            bytes_accessed=2 * count << 20,
            transcendentals=count * GROUP * tok * 1280,
        ),
        name="attend",
    )(own, queries, before, top, bot, after, far, *extra)


def on_device(queries, keys, values, proj_weight):
    peers = lax.axis_size("ctx")
    me = lax.axis_index("ctx")
    bit = lambda b: (me & b) // b
    own_head = sum(bit(b) << s for s, b in enumerate(HEAD_BITS))
    own = jnp.stack(
        [own_head, bit(HALF_BIT), (me > 0).astype(jnp.int32), (me < peers - 1).astype(jnp.int32)]
    ).astype(jnp.int32)
    b0, b1, b2 = HEAD_BITS
    up = [(i, i + 1) for i in range(peers - 1)]
    down = [(i + 1, i) for i in range(peers - 1)]
    top1, bot1, sent = project(KV // 2, own, keys, values, proj_weight)
    top0, bot0, kept = project(0, own, keys, values, proj_weight)
    before0 = lax.ppermute(bot1, "ctx", up)
    after0 = lax.ppermute(top1, "ctx", down)
    part = merge([kept, swap(sent, b2)])
    blocks = [(place, half) for place in range(KV // 2) for half in range(2)]
    cut = lambda place, half: part[place : place + 1, :, half * HD : (half + 1) * HD]
    pieces = {block: cut(*block) for block in blocks}
    late = [block for block in blocks if block[1]]
    target = lambda place, half: b0 * (place & 1) ^ b1 * (place >> 1) ^ HALF_BIT * half
    first = [swap(pieces[block], target(*block)) for block in blocks[2::2]]
    held = lax.optimization_barrier(([pieces[x] for x in late], first[0], before0, after0))
    _, first[0], before0, after0 = held
    second = [swap(x, target(*block)) for x, block in zip(held[0], late)]
    arrived = [pieces[0, 0]] + first + second
    part = merge(arrived)
    rest = 1
    while rest < peers:
        if rest not in HEAD_BITS + (HALF_BIT,):
            part = merge([part, swap(part, rest)])
        rest *= 2
    far = (part[:, : 2 * HD] / part[:, T_ROW : T_ROW + 1]).astype(jnp.bfloat16)[:, None]
    at0 = jnp.concatenate([far, swap(far, HALF_BIT)], axis=1)
    near0 = (before0, top0, bot0, after0)
    at0, bot_sent, top_sent = lax.optimization_barrier((at0, bot0, top0))
    at1 = swap(at0, b0)
    before1 = lax.ppermute(bot_sent, "ctx", up)
    after1 = lax.ppermute(top_sent, "ctx", down)
    out = attend(0, own, queries, *near0, at0)
    at1, out = lax.optimization_barrier((at1, out))
    at01 = jnp.concatenate([at0, at1], axis=0)
    at23 = swap(at01, b1)
    out = attend(1, own, queries, *near0, at1, out)
    at23, out, before1, after1 = lax.optimization_barrier((at23, out, before1, after1))
    near1 = (before1, top1, bot1, after1)
    at4567 = swap(jnp.concatenate([at01, at23], axis=0), b2)
    out = attend(2, own, queries, *near0, at23, out)
    return attend(4, own, queries, *near1, at4567, out)


def solution(mesh):
    in_specs = (P("ctx", None), P("ctx", None), P("ctx", None), P())
    out_specs = P("ctx", None)
    return jax.shard_map(
        on_device, mesh=mesh, in_specs=in_specs, out_specs=out_specs, check_vma=False
    )
```

```python
import functools
import math

import jax
import jax.numpy as jnp
from jax import lax
from jax.experimental import pallas as pl
from jax.experimental.pallas import tpu as pltpu
from jax.sharding import PartitionSpec as P

H = 32
KV = 8
HD = 128
GROUP = H // KV
R = 256
HALF = 256
AUX = 8
ROWS = 2 * HD + AUX
T_ROW = 2 * HD
M_ROW = 2 * HD + 1
EXP2_SCALE = math.log2(math.e) / math.sqrt(HD)
FAR_AWAY = 1e30
BLOCKS = 5
PROJECT_VMEM = 60 << 20
ATTEND_VMEM = 48 << 20

HEAD_BITS = (4, 2, 1)
HALF_BIT = 8
CORE_BIT = 1


def normalize(x):
    centered = x - jnp.mean(x, axis=-1, keepdims=True)
    spread = jnp.mean(centered * centered, axis=-1, keepdims=True)
    return centered * lax.rsqrt(spread + 1e-05)


def project_kernel(own, k_ref, v_ref, w0_ref, w1_ref, in_ref, out_ref, part_ref):
    for i in range(2):
        side = (i ^ own[0]) & 1
        lane = pl.multiple_of(side * HD, HD)
        keys = k_ref[:, pl.ds(lane, HD)]
        values = v_ref[:, pl.ds(lane, HD)]
        near_k = normalize(keys.astype(jnp.float32)).astype(jnp.bfloat16)
        near_v = normalize(values.astype(jnp.float32)).astype(jnp.bfloat16)
        near = jnp.concatenate([near_k, near_v], axis=1)
        wide = pl.multiple_of(side * 2 * HD, 2 * HD)
        odd = own[2] > 0
        in_ref[:, pl.ds(wide, 2 * HD)] = jnp.where(odd, near[:HALF], near[HALF:])
        out_ref[:, pl.ds(wide, 2 * HD)] = jnp.where(odd, near[HALF:], near[:HALF])
        weight = jnp.concatenate([w0_ref[side], w1_ref[side]], axis=1)
        logits = jnp.dot(near_k, weight, preferred_element_type=jnp.float32)
        top = jnp.max(logits, axis=0, keepdims=True)
        expo = jnp.exp(logits - top)
        total = jnp.sum(expo, axis=0, keepdims=True)
        upper = expo.astype(jnp.bfloat16)
        lower = (expo - upper.astype(jnp.float32)).astype(jnp.bfloat16)
        pair = jnp.concatenate([keys, values], axis=1)
        dims = (((0,), (0,)), ((), ()))
        both = lax.dot_general(pair, upper, dims, preferred_element_type=jnp.float32)
        both = both + lax.dot_general(pair, lower, dims, preferred_element_type=jnp.float32)
        part_ref[i, : 2 * HD] = both
        row = lax.broadcasted_iota(jnp.int32, (AUX, R), 0)
        part_ref[i, 2 * HD :] = jnp.where(row == 0, total, jnp.where(row == 1, top, 0.0))


def project(base, own, keys, values, proj_weight):
    tok = keys.shape[0]
    two = lambda i, own: (base + 2 * i ^ own[0]) // 2
    count = KV // 2
    wide = pl.BlockSpec((HALF, 4 * HD), lambda i, own: (0, two(i, own) % (count // 2)))
    return pl.pallas_call(
        project_kernel,
        out_shape=(
            jax.ShapeDtypeStruct((HALF, count * 2 * HD), jnp.bfloat16),
            jax.ShapeDtypeStruct((HALF, count * 2 * HD), jnp.bfloat16),
            jax.ShapeDtypeStruct((count, ROWS, R), jnp.float32),
        ),
        grid_spec=pltpu.PrefetchScalarGridSpec(
            num_scalar_prefetch=1,
            grid=(count // 2,),
            in_specs=[
                pl.BlockSpec((tok, 2 * HD), lambda i, own: (0, two(i, own))),
                pl.BlockSpec((tok, 2 * HD), lambda i, own: (0, two(i, own))),
                pl.BlockSpec((2, HD, R // 2), lambda i, own: (two(i, own), 0, own[1])),
                pl.BlockSpec((2, HD, R // 2), lambda i, own: (two(i, own), 0, 1 - own[1])),
            ],
            out_specs=[wide, wide, pl.BlockSpec((2, ROWS, R), lambda i, own: (i, 0, 0))],
        ),
        compiler_params=pltpu.CompilerParams(vmem_limit_bytes=PROJECT_VMEM),
        cost_estimate=pl.CostEstimate(
            flops=count * tok * R * HD * 10, bytes_accessed=4 << 20, transcendentals=count * tok * R
        ),
        name="project",
    )(own, keys, values, proj_weight, proj_weight)


def merge(parts):
    tops = [x[:, M_ROW : M_ROW + 1] for x in parts]
    top = functools.reduce(jnp.maximum, tops)
    row = lax.broadcasted_iota(jnp.int32, parts[0].shape, 1)
    added = sum(x * jnp.exp(t - top) for x, t in zip(parts, tops))
    return jnp.where(row == M_ROW, top, added)


def swap(x, bits):
    peers = lax.axis_size("ctx")
    return lax.ppermute(x, "ctx", [(i, i ^ bits) for i in range(peers)])


def attend_kernel(own, q_ref, a_ref, b_ref, in_ref, out_ref, g_ref, *refs):
    o_ref, k_ref, v_ref = refs[-3:]
    hide = (0.0, 0.0, 0.0, jnp.where(own[3] > 0, 0.0, FAR_AWAY), 0.0)
    for i, x in enumerate((a_ref, b_ref, in_ref, out_ref)):
        k_ref[i * HALF : (i + 1) * HALF] = x[:, :HD]
        v_ref[:, i * HALF : (i + 1) * HALF] = x[:, HD:].T
    for i in range(2):
        at = 4 * HALF + i * HD
        k_ref[at : at + HD] = g_ref[0, i, :HD].T
        v_ref[:, at : at + HD] = g_ref[0, i, HD:]
    flip = (((1,), (1,)), ((), ()))

    def score(g, i):
        return lax.dot_general(
            k_ref[i * HALF : (i + 1) * HALF],
            q_ref[:, g * HD : (g + 1) * HD],
            flip,
            preferred_element_type=jnp.float32,
        )

    scores = [score(0, i) for i in range(BLOCKS)]
    for g in range(GROUP):
        tops = [jnp.max(s, axis=0, keepdims=True) - w for s, w in zip(scores, hide)]
        top = functools.reduce(jnp.maximum, tops)
        ahead, expo, total = [], [], 0.0
        for i in range(BLOCKS):
            if g + 1 < GROUP:
                ahead.append(score(g + 1, i))
            e = jnp.exp2((scores[i] - (top + hide[i])) * EXP2_SCALE)
            total = total + jnp.sum(e, axis=0, keepdims=True)
            expo.append(e)
        inverse = 1.0 / total
        probs = jnp.concatenate([(e * inverse).astype(jnp.bfloat16) for e in expo], axis=0)
        mixed = jnp.dot(v_ref[...], probs, preferred_element_type=jnp.float32)
        o_ref[:, g * HD : (g + 1) * HD] = mixed.T.astype(jnp.bfloat16)
        scores = ahead


def attend(base, own, queries, nears, far, out=None):
    tok = queries.shape[0]
    count = far.shape[0]
    head = lambda i, own: base + i ^ own[0]
    place = lambda i, own: head(i, own) % (KV // 2)
    edge = pl.BlockSpec((HALF, 2 * HD), lambda i, own: (0, place(i, own)))
    extra = [] if out is None else [out]
    return pl.pallas_call(
        attend_kernel,
        out_shape=jax.ShapeDtypeStruct(queries.shape, jnp.bfloat16),
        grid_spec=pltpu.PrefetchScalarGridSpec(
            num_scalar_prefetch=1,
            grid=(count,),
            in_specs=[
                pl.BlockSpec((tok, GROUP * HD), lambda i, own: (0, head(i, own))),
                edge,
                edge,
                edge,
                edge,
                pl.BlockSpec((1, 2, 2 * HD, R // 2), lambda i, own: (i, 0, 0, 0)),
            ]
            + [pl.BlockSpec(memory_space=pl.ANY)] * len(extra),
            out_specs=pl.BlockSpec((tok, GROUP * HD), lambda i, own: (0, head(i, own))),
            scratch_shapes=[
                pltpu.VMEM((BLOCKS * HALF, HD), jnp.bfloat16),
                pltpu.VMEM((HD, BLOCKS * HALF), jnp.bfloat16),
            ],
        ),
        input_output_aliases={7: 0} if extra else {},
        compiler_params=pltpu.CompilerParams(vmem_limit_bytes=ATTEND_VMEM),
        cost_estimate=pl.CostEstimate(
            flops=4 * count * GROUP * tok * 1280 * HD,
            bytes_accessed=2 * count << 20,
            transcendentals=count * GROUP * tok * 1280,
        ),
        name="attend",
    )(own, queries, *nears, far, *extra)


def on_device(queries, keys, values, proj_weight):
    peers = lax.axis_size("ctx")
    me = lax.axis_index("ctx")
    bit = lambda b: (me & b) // b
    own_head = sum(bit(b) << s for s, b in enumerate(HEAD_BITS))
    edge = (me == 0) | (me == peers - 1)
    own = jnp.stack([own_head, bit(HALF_BIT), bit(CORE_BIT), 1 - edge]).astype(jnp.int32)
    b0, b1, b2 = HEAD_BITS
    across = [(i, i + 1) for i in range(1, peers - 1, 2)]
    across = across + [(j, i) for i, j in across]
    in1, out1, sent = project(KV // 2, own, keys, values, proj_weight)
    in0, out0, kept = project(0, own, keys, values, proj_weight)
    outer0 = lax.ppermute(out1, "ctx", across)
    inner0 = swap(in1, CORE_BIT)
    outer1 = lax.ppermute(out0, "ctx", across)
    inner1 = swap(in0, CORE_BIT)
    part = merge([kept, swap(sent, b2)])
    blocks = [(place, half) for place in range(KV // 2) for half in range(2)]
    target = lambda place, half: b0 * (place & 1) ^ b1 * (place >> 1) ^ HALF_BIT * half
    cut = lambda place, half: part[place : place + 1, :, half * HD : (half + 1) * HD]
    first = [swap(cut(*block), target(*block)) for block in blocks[1:4]]
    late = [cut(*block) for block in blocks[4:]]
    late, first[0], outer0 = lax.optimization_barrier((late, first[0], outer0))
    second = [swap(x, target(*block)) for x, block in zip(late, blocks[4:])]
    part = merge([cut(0, 0)] + first + second)
    rest = 1
    while rest < peers:
        if rest not in HEAD_BITS + (HALF_BIT,):
            part = merge([part, swap(part, rest)])
        rest *= 2
    far = (part[:, : 2 * HD] / part[:, T_ROW : T_ROW + 1]).astype(jnp.bfloat16)[:, None]
    at0 = jnp.concatenate([far, swap(far, HALF_BIT)], axis=1)
    at1 = swap(at0, b0)
    nears0 = (in0, out0, inner0, outer0)
    out = attend(0, own, queries, nears0, at0)
    at1, out, outer1 = lax.optimization_barrier((at1, out, outer1))
    at01 = jnp.concatenate([at0, at1], axis=0)
    at23 = swap(at01, b1)
    out = attend(1, own, queries, nears0, at1, out)
    at23, out = lax.optimization_barrier((at23, out))
    at4567 = swap(jnp.concatenate([at01, at23], axis=0), b2)
    nears1 = (in1, out1, inner1, outer1)
    out = attend(2, own, queries, nears0, at23, out)
    return attend(4, own, queries, nears1, at4567, out)


def solution(mesh):
    in_specs = (P("ctx", None), P("ctx", None), P("ctx", None), P())
    out_specs = P("ctx", None)
    return jax.shard_map(
        on_device, mesh=mesh, in_specs=in_specs, out_specs=out_specs, check_vma=False
    )
```

```python
import functools
import math

import jax
import jax.numpy as jnp
from jax import lax
from jax.experimental import pallas as pl
from jax.experimental.pallas import tpu as pltpu
from jax.sharding import PartitionSpec as P

H = 32
KV = 8
HD = 128
GROUP = H // KV
R = 256
HALF = 256
AUX = 8
ROWS = 2 * HD + AUX
T_ROW = 2 * HD
M_ROW = 2 * HD + 1
EXP2_SCALE = math.log2(math.e) / math.sqrt(HD)
FAR_AWAY = 1e30
BLOCKS = 5
PROJECT_VMEM = 16 << 20
ATTEND_VMEM = 24 << 20

HEAD_BITS = (4, 2, 1)
HALF_BIT = 8
CORE_BIT = 1


def normalize(x):
    centered = x - jnp.mean(x, axis=-1, keepdims=True)
    spread = jnp.mean(centered * centered, axis=-1, keepdims=True)
    return centered * lax.rsqrt(spread + 1e-05)


def project_kernel(own, k_ref, v_ref, w0_ref, w1_ref, in_ref, out_ref, part_ref):
    for i in range(2):
        side = (i ^ own[0]) & 1
        lane = pl.multiple_of(side * HD, HD)
        keys = k_ref[:, pl.ds(lane, HD)]
        values = v_ref[:, pl.ds(lane, HD)]
        near_k = normalize(keys.astype(jnp.float32)).astype(jnp.bfloat16)
        near_v = normalize(values.astype(jnp.float32)).astype(jnp.bfloat16)
        near = jnp.concatenate([near_k, near_v], axis=1)
        wide = pl.multiple_of(side * 2 * HD, 2 * HD)
        odd = own[2] > 0
        in_ref[:, pl.ds(wide, 2 * HD)] = jnp.where(odd, near[:HALF], near[HALF:])
        out_ref[:, pl.ds(wide, 2 * HD)] = jnp.where(odd, near[HALF:], near[:HALF])
        weight = jnp.concatenate([w0_ref[side], w1_ref[side]], axis=1)
        logits = jnp.dot(near_k, weight, preferred_element_type=jnp.float32)
        top = jnp.max(logits, axis=0, keepdims=True)
        expo = jnp.exp(logits - top)
        total = jnp.sum(expo, axis=0, keepdims=True)
        upper = expo.astype(jnp.bfloat16)
        lower = (expo - upper.astype(jnp.float32)).astype(jnp.bfloat16)
        pair = jnp.concatenate([keys, values], axis=1)
        dims = (((0,), (0,)), ((), ()))
        split = jnp.concatenate([upper, lower], axis=1)
        both = lax.dot_general(pair, split, dims, preferred_element_type=jnp.float32)
        both = both[:, :R] + both[:, R:]
        part_ref[i, : 2 * HD] = both
        row = lax.broadcasted_iota(jnp.int32, (AUX, R), 0)
        part_ref[i, 2 * HD :] = jnp.where(row == 0, total, jnp.where(row == 1, top, 0.0))


def project(base, own, keys, values, proj_weight):
    tok = keys.shape[0]
    two = lambda i, own: (base + 2 * i ^ own[0]) // 2
    count = KV // 2
    wide = pl.BlockSpec((HALF, 4 * HD), lambda i, own: (0, two(i, own) % (count // 2)))
    return pl.pallas_call(
        project_kernel,
        out_shape=(
            jax.ShapeDtypeStruct((HALF, count * 2 * HD), jnp.bfloat16),
            jax.ShapeDtypeStruct((HALF, count * 2 * HD), jnp.bfloat16),
            jax.ShapeDtypeStruct((count, ROWS, R), jnp.float32),
        ),
        grid_spec=pltpu.PrefetchScalarGridSpec(
            num_scalar_prefetch=1,
            grid=(count // 2,),
            in_specs=[
                pl.BlockSpec((tok, 2 * HD), lambda i, own: (0, two(i, own))),
                pl.BlockSpec((tok, 2 * HD), lambda i, own: (0, two(i, own))),
                pl.BlockSpec((2, HD, R // 2), lambda i, own: (two(i, own), 0, own[1])),
                pl.BlockSpec((2, HD, R // 2), lambda i, own: (two(i, own), 0, 1 - own[1])),
            ],
            out_specs=[wide, wide, pl.BlockSpec((2, ROWS, R), lambda i, own: (i, 0, 0))],
        ),
        compiler_params=pltpu.CompilerParams(vmem_limit_bytes=PROJECT_VMEM),
        cost_estimate=pl.CostEstimate(
            flops=count * tok * R * HD * 10, bytes_accessed=4 << 20, transcendentals=count * tok * R
        ),
        name="project",
    )(own, keys, values, proj_weight, proj_weight)


def merge(parts):
    tops = [x[:, M_ROW : M_ROW + 1] for x in parts]
    top = functools.reduce(jnp.maximum, tops)
    row = lax.broadcasted_iota(jnp.int32, parts[0].shape, 1)
    added = sum(x * jnp.exp(t - top) for x, t in zip(parts, tops))
    return jnp.where(row == M_ROW, top, added)


def swap(x, bits):
    peers = lax.axis_size("ctx")
    return lax.ppermute(x, "ctx", [(i, i ^ bits) for i in range(peers)])


def attend_kernel(per, own, q_ref, a_ref, b_ref, in_ref, out_ref, g_ref, *refs):
    o_ref, k_ref, v_ref = refs[-3:]
    hide = (0.0, 0.0, 0.0, jnp.where(own[3] > 0, 0.0, FAR_AWAY), 0.0)
    flip = (((1,), (1,)), ((), ()))
    sides = [(h ^ own[0]) & (per - 1) for h in range(per)]

    def columns(h, start, width, size):
        if per == 1:
            return slice(start, start + width)
        return pl.ds(pl.multiple_of(sides[h] * size + start, HD), width)

    def load(h):
        for i, x in enumerate((a_ref, b_ref, in_ref, out_ref)):
            k_ref[h, i * HALF : (i + 1) * HALF] = x[:, columns(h, 0, HD, 2 * HD)]
            v_ref[h, :, i * HALF : (i + 1) * HALF] = x[:, columns(h, HD, HD, 2 * HD)].T
        for i in range(2):
            at = 4 * HALF + i * HD
            k_ref[h, at : at + HD] = g_ref[h, i, :HD].T
            v_ref[h, :, at : at + HD] = g_ref[h, i, HD:]

    def score(h, g, i):
        return lax.dot_general(
            k_ref[h, i * HALF : (i + 1) * HALF],
            q_ref[:, columns(h, g * HD, HD, GROUP * HD)],
            flip,
            preferred_element_type=jnp.float32,
        )

    load(0)
    tiles = [(h, g) for h in range(per) for g in range(GROUP)]
    scores = [score(0, 0, i) for i in range(BLOCKS)]
    for n, (h, g) in enumerate(tiles):
        if g == 1 and h + 1 < per:
            load(h + 1)
        tops = [jnp.max(s, axis=0, keepdims=True) - w for s, w in zip(scores, hide)]
        top = functools.reduce(jnp.maximum, tops)
        ahead, expo, total = [], [], 0.0
        for i in range(BLOCKS):
            if n + 1 < len(tiles):
                ahead.append(score(*tiles[n + 1], i))
            e = jnp.exp2((scores[i] - (top + hide[i])) * EXP2_SCALE)
            total = total + jnp.sum(e, axis=0, keepdims=True)
            expo.append(e)
        inverse = 1.0 / total
        probs = jnp.concatenate([(e * inverse).astype(jnp.bfloat16) for e in expo], axis=0)
        mixed = jnp.dot(v_ref[h], probs, preferred_element_type=jnp.float32)
        o_ref[:, columns(h, g * HD, HD, GROUP * HD)] = mixed.T.astype(jnp.bfloat16)
        scores = ahead


def attend(base, own, queries, nears, far, out=None, per=1):
    tok = queries.shape[0]
    count = far.shape[0]
    block = lambda i, own: (base + per * i ^ own[0]) // per
    edge = pl.BlockSpec(
        (HALF, per * 2 * HD), lambda i, own: (0, block(i, own) % (KV // 2 // per))
    )
    whole = pl.BlockSpec((tok, per * GROUP * HD), lambda i, own: (0, block(i, own)))
    extra = [] if out is None else [out]
    return pl.pallas_call(
        functools.partial(attend_kernel, per),
        out_shape=jax.ShapeDtypeStruct(queries.shape, jnp.bfloat16),
        grid_spec=pltpu.PrefetchScalarGridSpec(
            num_scalar_prefetch=1,
            grid=(count // per,),
            in_specs=[
                whole,
                edge,
                edge,
                edge,
                edge,
                pl.BlockSpec((per, 2, 2 * HD, R // 2), lambda i, own: (i, 0, 0, 0)),
            ]
            + [pl.BlockSpec(memory_space=pl.ANY)] * len(extra),
            out_specs=whole,
            scratch_shapes=[
                pltpu.VMEM((per, BLOCKS * HALF, HD), jnp.bfloat16),
                pltpu.VMEM((per, HD, BLOCKS * HALF), jnp.bfloat16),
            ],
        ),
        input_output_aliases={7: 0} if extra else {},
        compiler_params=pltpu.CompilerParams(vmem_limit_bytes=ATTEND_VMEM),
        cost_estimate=pl.CostEstimate(
            flops=4 * count * GROUP * tok * 1280 * HD,
            bytes_accessed=2 * count << 20,
            transcendentals=count * GROUP * tok * 1280,
        ),
        name="attend",
    )(own, queries, *nears, far, *extra)


def on_device(queries, keys, values, proj_weight):
    peers = lax.axis_size("ctx")
    me = lax.axis_index("ctx")
    bit = lambda b: (me & b) // b
    own_head = sum(bit(b) << s for s, b in enumerate(HEAD_BITS))
    edge = (me == 0) | (me == peers - 1)
    own = jnp.stack([own_head, bit(HALF_BIT), bit(CORE_BIT), 1 - edge]).astype(jnp.int32)
    b0, b1, b2 = HEAD_BITS
    across = [(i, i + 1) for i in range(1, peers - 1, 2)]
    across = across + [(j, i) for i, j in across]
    keys, values, proj_weight = [
        pltpu.with_memory_space_constraint(x, pltpu.HBM) for x in (keys, values, proj_weight)
    ]
    in1, out1, sent = project(KV // 2, own, keys, values, proj_weight)
    in0, out0, kept = project(0, own, keys, values, proj_weight)
    outer0 = lax.ppermute(out1, "ctx", across)
    inner0 = swap(in1, CORE_BIT)
    outer1 = lax.ppermute(out0, "ctx", across)
    inner1 = swap(in0, CORE_BIT)
    part = merge([kept, swap(sent, b2)])
    blocks = [(place, half) for place in range(KV // 2) for half in range(2)]
    target = lambda place, half: b0 * (place & 1) ^ b1 * (place >> 1) ^ HALF_BIT * half
    cut = lambda place, half: part[place : place + 1, :, half * HD : (half + 1) * HD]
    first = [swap(cut(*block), target(*block)) for block in blocks[1:4]]
    late = [cut(*block) for block in blocks[4:]]
    late, first[0], outer0 = lax.optimization_barrier((late, first[0], outer0))
    second = [swap(x, target(*block)) for x, block in zip(late, blocks[4:])]
    part = merge([cut(0, 0)] + first + second)
    rest = 1
    while rest < peers:
        if rest not in HEAD_BITS + (HALF_BIT,):
            part = merge([part, swap(part, rest)])
        rest *= 2
    far = (part[:, : 2 * HD] / part[:, T_ROW : T_ROW + 1]).astype(jnp.bfloat16)[:, None]
    at0 = jnp.concatenate([far, swap(far, HALF_BIT)], axis=1)
    at1 = swap(at0, b0)
    nears0 = (in0, out0, inner0, outer0)
    out = attend(0, own, queries, nears0, at0)
    at1, out, outer1 = lax.optimization_barrier((at1, out, outer1))
    at01 = jnp.concatenate([at0, at1], axis=0)
    at23 = swap(at01, b1)
    out = attend(1, own, queries, nears0, at1, out)
    at23, out = lax.optimization_barrier((at23, out))
    at4567 = swap(jnp.concatenate([at01, at23], axis=0), b2)
    nears1 = (in1, out1, inner1, outer1)
    out = attend(2, own, queries, nears0, at23, out, 2)
    return attend(4, own, queries, nears1, at4567, out, 2)


def solution(mesh):
    in_specs = (P("ctx", None), P("ctx", None), P("ctx", None), P())
    out_specs = P("ctx", None)
    return jax.shard_map(
        on_device, mesh=mesh, in_specs=in_specs, out_specs=out_specs, check_vma=False
    )
```

```python
import functools
import math

import jax
import jax.numpy as jnp
from jax import lax
from jax.experimental import pallas as pl
from jax.experimental.pallas import tpu as pltpu
from jax.sharding import PartitionSpec as P

H = 32
KV = 8
HD = 128
GROUP = H // KV
R = 256
HALF = 256
AUX = 8
ROWS = 2 * HD + AUX
T_ROW = 2 * HD
M_ROW = 2 * HD + 1
EXP2_SCALE = math.log2(math.e) / math.sqrt(HD)
FAR_AWAY = 1e30
BLOCKS = 5
PROJECT_VMEM = 16 << 20
ATTEND_VMEM = 24 << 20

HEAD_BITS = (4, 2, 1)
HALF_BIT = 8
CORE_BIT = 1


def normalize(x):
    centered = x - jnp.mean(x, axis=-1, keepdims=True)
    spread = jnp.mean(centered * centered, axis=-1, keepdims=True)
    return centered * lax.rsqrt(spread + 1e-05)


def project_kernel(own, k_ref, v_ref, w0_ref, w1_ref, in_ref, out_ref, part_ref):
    for i in range(2):
        side = (i ^ own[0]) & 1
        lane = pl.multiple_of(side * HD, HD)
        keys = k_ref[:, pl.ds(lane, HD)]
        values = v_ref[:, pl.ds(lane, HD)]
        near_k = normalize(keys.astype(jnp.float32)).astype(jnp.bfloat16)
        near_v = normalize(values.astype(jnp.float32)).astype(jnp.bfloat16)
        near = jnp.concatenate([near_k, near_v], axis=1)
        wide = pl.multiple_of(side * 2 * HD, 2 * HD)
        odd = own[2] > 0
        in_ref[:, pl.ds(wide, 2 * HD)] = jnp.where(odd, near[:HALF], near[HALF:])
        out_ref[:, pl.ds(wide, 2 * HD)] = jnp.where(odd, near[HALF:], near[:HALF])
        weight = jnp.concatenate([w0_ref[side], w1_ref[side]], axis=1)
        logits = jnp.dot(near_k, weight, preferred_element_type=jnp.float32)
        top = jnp.max(logits, axis=0, keepdims=True)
        expo = jnp.exp(logits - top)
        total = jnp.sum(expo, axis=0, keepdims=True)
        upper = expo.astype(jnp.bfloat16)
        lower = (expo - upper.astype(jnp.float32)).astype(jnp.bfloat16)
        pair = jnp.concatenate([keys, values], axis=1)
        dims = (((0,), (0,)), ((), ()))
        split = jnp.concatenate([upper, lower], axis=1)
        both = lax.dot_general(pair, split, dims, preferred_element_type=jnp.float32)
        both = both[:, :R] + both[:, R:]
        part_ref[i, : 2 * HD] = both
        row = lax.broadcasted_iota(jnp.int32, (AUX, R), 0)
        part_ref[i, 2 * HD :] = jnp.where(row == 0, total, jnp.where(row == 1, top, 0.0))


def project(base, own, keys, values, proj_weight):
    tok = keys.shape[0]
    two = lambda i, own: (base + 2 * i ^ own[0]) // 2
    count = KV // 2
    wide = pl.BlockSpec((HALF, 4 * HD), lambda i, own: (0, two(i, own) % (count // 2)))
    return pl.pallas_call(
        project_kernel,
        out_shape=(
            jax.ShapeDtypeStruct((HALF, count * 2 * HD), jnp.bfloat16),
            jax.ShapeDtypeStruct((HALF, count * 2 * HD), jnp.bfloat16),
            jax.ShapeDtypeStruct((count, ROWS, R), jnp.float32),
        ),
        grid_spec=pltpu.PrefetchScalarGridSpec(
            num_scalar_prefetch=1,
            grid=(count // 2,),
            in_specs=[
                pl.BlockSpec((tok, 2 * HD), lambda i, own: (0, two(i, own))),
                pl.BlockSpec((tok, 2 * HD), lambda i, own: (0, two(i, own))),
                pl.BlockSpec((2, HD, R // 2), lambda i, own: (two(i, own), 0, own[1])),
                pl.BlockSpec((2, HD, R // 2), lambda i, own: (two(i, own), 0, 1 - own[1])),
            ],
            out_specs=[wide, wide, pl.BlockSpec((2, ROWS, R), lambda i, own: (i, 0, 0))],
        ),
        compiler_params=pltpu.CompilerParams(vmem_limit_bytes=PROJECT_VMEM),
        cost_estimate=pl.CostEstimate(
            flops=count * tok * R * HD * 10, bytes_accessed=4 << 20, transcendentals=count * tok * R
        ),
        name="project",
    )(own, keys, values, proj_weight, proj_weight)


def merge(parts):
    tops = [x[:, M_ROW : M_ROW + 1] for x in parts]
    top = functools.reduce(jnp.maximum, tops)
    row = lax.broadcasted_iota(jnp.int32, parts[0].shape, 1)
    added = sum(x * jnp.exp(t - top) for x, t in zip(parts, tops))
    return jnp.where(row == M_ROW, top, added)


def swap(x, bits):
    peers = lax.axis_size("ctx")
    return lax.ppermute(x, "ctx", [(i, i ^ bits) for i in range(peers)])


def attend_kernel(per, own, q_ref, a_ref, b_ref, in_ref, out_ref, g_ref, *refs):
    o_ref, k_ref, v_ref = refs[-3:]
    hide = (0.0, 0.0, 0.0, jnp.where(own[3] > 0, 0.0, FAR_AWAY), 0.0)
    flip = (((1,), (1,)), ((), ()))
    sides = [(h ^ own[0]) & (per - 1) for h in range(per)]

    def columns(h, start, width, size):
        if per == 1:
            return slice(start, start + width)
        return pl.ds(pl.multiple_of(sides[h] * size + start, HD), width)

    def load(h):
        for i, x in enumerate((a_ref, b_ref, in_ref, out_ref)):
            k_ref[h, i * HALF : (i + 1) * HALF] = x[:, columns(h, 0, HD, 2 * HD)]
            v_ref[h, :, i * HALF : (i + 1) * HALF] = x[:, columns(h, HD, HD, 2 * HD)].T
        for i in range(2):
            at = 4 * HALF + i * HD
            k_ref[h, at : at + HD] = g_ref[h, i, :HD].T
            v_ref[h, :, at : at + HD] = g_ref[h, i, HD:]

    def score(h, g, i):
        return lax.dot_general(
            k_ref[h, i * HALF : (i + 1) * HALF],
            q_ref[:, columns(h, g * HD, HD, GROUP * HD)],
            flip,
            preferred_element_type=jnp.float32,
        )

    load(0)
    tiles = [(h, g) for h in range(per) for g in range(GROUP)]
    scores = [score(0, 0, i) for i in range(BLOCKS)]
    for n, (h, g) in enumerate(tiles):
        if g == 1 and h + 1 < per:
            load(h + 1)
        tops = [jnp.max(s, axis=0, keepdims=True) - w for s, w in zip(scores, hide)]
        top = functools.reduce(jnp.maximum, tops)
        ahead, expo, total = [], [], 0.0
        for i in range(BLOCKS):
            if n + 1 < len(tiles):
                ahead.append(score(*tiles[n + 1], i))
            e = jnp.exp2((scores[i] - (top + hide[i])) * EXP2_SCALE)
            total = total + jnp.sum(e, axis=0, keepdims=True)
            expo.append(e)
        inverse = 1.0 / total
        probs = jnp.concatenate([(e * inverse).astype(jnp.bfloat16) for e in expo], axis=0)
        mixed = jnp.dot(v_ref[h], probs, preferred_element_type=jnp.float32)
        o_ref[:, columns(h, g * HD, HD, GROUP * HD)] = mixed.T.astype(jnp.bfloat16)
        scores = ahead


def attend(base, own, queries, nears, far, out=None, per=1):
    tok = queries.shape[0]
    count = far.shape[0]
    block = lambda i, own: (base + per * i ^ own[0]) // per
    edge = pl.BlockSpec(
        (HALF, per * 2 * HD), lambda i, own: (0, block(i, own) % (KV // 2 // per))
    )
    whole = pl.BlockSpec((tok, per * GROUP * HD), lambda i, own: (0, block(i, own)))
    extra = [] if out is None else [out]
    return pl.pallas_call(
        functools.partial(attend_kernel, per),
        out_shape=jax.ShapeDtypeStruct(queries.shape, jnp.bfloat16),
        grid_spec=pltpu.PrefetchScalarGridSpec(
            num_scalar_prefetch=1,
            grid=(count // per,),
            in_specs=[
                whole,
                edge,
                edge,
                edge,
                edge,
                pl.BlockSpec((per, 2, 2 * HD, R // 2), lambda i, own: (i, 0, 0, 0)),
            ]
            + [pl.BlockSpec(memory_space=pl.ANY)] * len(extra),
            out_specs=whole,
            scratch_shapes=[
                pltpu.VMEM((per, BLOCKS * HALF, HD), jnp.bfloat16),
                pltpu.VMEM((per, HD, BLOCKS * HALF), jnp.bfloat16),
            ],
        ),
        input_output_aliases={7: 0} if extra else {},
        compiler_params=pltpu.CompilerParams(vmem_limit_bytes=ATTEND_VMEM),
        cost_estimate=pl.CostEstimate(
            flops=4 * count * GROUP * tok * 1280 * HD,
            bytes_accessed=2 * count << 20,
            transcendentals=count * GROUP * tok * 1280,
        ),
        name="attend",
    )(own, queries, *nears, far, *extra)


def on_device(queries, keys, values, proj_weight):
    peers = lax.axis_size("ctx")
    me = lax.axis_index("ctx")
    bit = lambda b: (me & b) // b
    own_head = sum(bit(b) << s for s, b in enumerate(HEAD_BITS))
    edge = (me == 0) | (me == peers - 1)
    own = jnp.stack([own_head, bit(HALF_BIT), bit(CORE_BIT), 1 - edge]).astype(jnp.int32)
    b0, b1, b2 = HEAD_BITS
    across = [(i, i + 1) for i in range(1, peers - 1, 2)]
    across = across + [(j, i) for i, j in across]
    keys, values, proj_weight = [
        pltpu.with_memory_space_constraint(x, pltpu.HBM) for x in (keys, values, proj_weight)
    ]
    in1, out1, sent = project(KV // 2, own, keys, values, proj_weight)
    in0, out0, kept = project(0, own, keys, values, proj_weight)
    outer0 = lax.ppermute(out1, "ctx", across)
    inner0 = swap(in1, CORE_BIT)
    outer1 = lax.ppermute(out0, "ctx", across)
    inner1 = swap(in0, CORE_BIT)
    part = merge([kept, swap(sent, b2)])
    blocks = [(place, half) for place in range(KV // 2) for half in range(2)]
    target = lambda place, half: b0 * (place & 1) ^ b1 * (place >> 1) ^ HALF_BIT * half
    cut = lambda place, half: part[place : place + 1, :, half * HD : (half + 1) * HD]
    first = [swap(cut(*block), target(*block)) for block in blocks[1:4]]
    late = [cut(*block) for block in blocks[4:]]
    late, first[0], outer0 = lax.optimization_barrier((late, first[0], outer0))
    second = [swap(x, target(*block)) for x, block in zip(late, blocks[4:])]
    part = merge([cut(0, 0)] + first + second)
    part, inner0, inner1 = lax.optimization_barrier((part, inner0, inner1))
    rest = 1
    while rest < peers:
        if rest not in HEAD_BITS + (HALF_BIT,):
            part = merge([part, swap(part, rest)])
        rest *= 2
    far = (part[:, : 2 * HD] / part[:, T_ROW : T_ROW + 1]).astype(jnp.bfloat16)[:, None]
    at0 = jnp.concatenate([far, swap(far, HALF_BIT)], axis=1)
    at1 = swap(at0, b0)
    nears0 = (in0, out0, inner0, outer0)
    out = attend(0, own, queries, nears0, at0)
    at1, out, outer1 = lax.optimization_barrier((at1, out, outer1))
    at01 = jnp.concatenate([at0, at1], axis=0)
    at23 = swap(at01, b1)
    at45 = swap(at01, b2)
    out = attend(1, own, queries, nears0, at1, out)
    nears1 = (in1, out1, inner1, outer1)
    out = attend(4, own, queries, nears1, at45, out, 2)
    at23, out = lax.optimization_barrier((at23, out))
    at67 = swap(at23, b2)
    out = attend(2, own, queries, nears0, at23, out, 2)
    return attend(6, own, queries, nears1, at67, out, 2)


def solution(mesh):
    in_specs = (P("ctx", None), P("ctx", None), P("ctx", None), P())
    out_specs = P("ctx", None)
    return jax.shard_map(
        on_device, mesh=mesh, in_specs=in_specs, out_specs=out_specs, check_vma=False
    )
```
